256 devices in a mesh: tm: 32 (over y, x, core), tensor: 8 (over z).
Axes of the slice: x: 4, y: 4, z: 8, core: 2. Of those that a mesh axis runs over, the one named last changes fastest.
Arguments:
- tokens: bfloat16 [32, 768, 2048], P('tm', None, 'tensor'), may hold values from -12 to 12
- action_rows: bfloat16 [32, 2048], P('tm', 'tensor'), may hold values from -6 to 6
- pair_index: int32 [32], P('tm'), may hold values from 0 to 31, each once
- episode_id: int32 [32], replicated, may hold values from 0 to 3, never falling along the last dimension, each value on 1 to 16 neighbouring positions
- space_gain: float32 [2048], replicated, may hold values from 0.25 to 1.75
- space_qkv: bfloat16 [3, 2048, 2048], P(None, None, 'tensor'), as said below
- space_out: bfloat16 [2048, 2048], P('tensor'), may hold values from -0.125 to 0.125
- time_gain: float32 [2048], replicated, may hold values from 0.25 to 1.75
- time_qkv: bfloat16 [3, 2048, 2048], P(None, None, 'tensor'), as said below
- time_out: bfloat16 [2048, 2048], P('tensor'), may hold values from -0.125 to 0.125
Outputs:
- result: bfloat16 [32, 768, 2048], P('tm', None, 'tensor')
The draws below stay inside these ranges and needn't reach their ends.
Inputs may be any that keep to these rules, and one draw needn't show every extreme that they name: pair_index names every encoder row exactly once. episode_id never falls along the frames; an episode has 1 to 16 frames. `space_qkv`: three stacked projection matrices, in the order query, key, value. `time_qkv`: three stacked projection matrices, in the order query, key, value.
All inputs are finite; a program needn't handle non-finite values.
Results may differ from the reference program's by a relative error of at most 0.012.
Values may be sent and summed in bfloat16 or wider, within the bound.
A program may use at most 64 MiB of HBM per device.

```python
import math
import jax
import jax.numpy as jnp
import numpy as np
from jax import lax

D = 2048
HEADS = 16
HEAD_DIM = 128
FRAME_TOKENS = 768
FRAMES = 32
EPISODES = 4


def stacked_projections(key):
    key_query, key_keys, key_values = jax.random.split(key, 3)
    shape_out = (D, HEADS * HEAD_DIM)
    query = jax.random.normal(key_query, shape_out, jnp.float32) * D ** (-0.5)
    noise = jax.random.normal(key_keys, shape_out, jnp.float32) * D ** (-0.5)
    values = jax.random.normal(key_values, shape_out, jnp.float32) * D ** (-0.5)
    keys = noise
    return jnp.stack([query, keys, values]).astype(jnp.bfloat16)


def draw_space_qkv(key, part):
    return stacked_projections(jax.random.fold_in(key, 11))


def draw_time_qkv(key, part):
    return stacked_projections(jax.random.fold_in(key, 23))


def draw_tokens(key, part):
    inner = jax.random.fold_in(key, 37)
    shape_all = (FRAMES, FRAME_TOKENS, D)
    place = jnp.arange(D, dtype=jnp.float32) / max(D - 1, 1)
    ramp = 0.3 * jnp.exp(place * jnp.log(10.0))
    values = jnp.clip(jax.random.normal(inner, shape_all, jnp.float32), -4.0, 4.0)
    return (values * ramp).astype(jnp.bfloat16)


def shard_levels(own_key, extent, pieces, low, high):
    level, own = 1.0, jax.random.fold_in(own_key, 6)
    for axis_at, shards_of in pieces:
        steps = jnp.exp(jax.random.uniform(jax.random.fold_in(own, axis_at), (shards_of,), jnp.float32, low / len(pieces), high / len(pieces)))
        level = level * jnp.repeat(steps, extent[axis_at] // shards_of).reshape([-1 if axis == axis_at else 1 for axis in range(len(extent))])
    return level


def length_profile(amount, total, bound, lean):
    portions = [(1 << 20) // math.isqrt(grade ** lean) + 1 for grade in range(2, amount + 1)]
    rest, counts = total - bound - (amount - 1), [1] * (amount - 1)
    while rest > 0:
        movable = [i for i in range(amount - 1) if counts[i] < bound]
        mass, remaining = sum([portions[i] for i in movable]), rest
        for i in movable:
            addition = min(bound - counts[i], max(1, remaining * portions[i] // mass), rest)
            counts[i] = counts[i] + addition
            rest = rest - addition
    return np.array([bound] + counts)


def uneven(stream_key, count, total, limit, lean):
    if count == 2:
        one = jax.random.randint(stream_key, (), max(1, total - limit), min(limit, total - 1) + 1)
        return jnp.stack([one, total - one])
    sizes = jnp.asarray(length_profile(count, total, limit, lean), jnp.int32)
    twos = (count - 1) // 2
    giver, receiver = sizes[1:1 + 2 * twos:2], sizes[2:2 + 2 * twos:2]
    room = jnp.minimum(giver - 1, limit - receiver)
    passed = jax.random.randint(jax.random.fold_in(stream_key, 1), (twos,), 0, 1 << 20) % (room + 1)
    sizes = sizes.at[1:1 + 2 * twos:2].set(giver - passed).at[2:2 + 2 * twos:2].set(receiver + passed)
    return sizes[jax.random.permutation(jax.random.fold_in(stream_key, 2), count)]


def centred(stream_key, extent, spread, reach, cuts=(), kind=jnp.bfloat16):
    factor_of = shard_levels(stream_key, extent, cuts, -0.22, 0.18) if cuts else 1.0
    drawn = jax.random.normal(stream_key, extent, jnp.float32) * spread * factor_of
    return jnp.minimum(jnp.maximum(drawn, -reach), reach).astype(kind)


def setup_inputs(seed: int = 0) -> dict:
    arg_keys = jax.random.split(jax.random.key(seed), 11)
    tokens = draw_tokens(jax.random.fold_in(arg_keys[10], 71), 0)
    action_rows = centred(arg_keys[1], (FRAMES, D), 1.0, 6.0, ((0, 32), (1, 8)))
    pair_index = jax.random.permutation(arg_keys[2], FRAMES).astype(jnp.int32)
    episode_id = jnp.searchsorted(jnp.cumsum(uneven(arg_keys[3], EPISODES, FRAMES, FRAMES // 2, 1)), jnp.arange(FRAMES), side="right").astype(jnp.int32)
    space_gain = jnp.clip(1.0 + 0.15 * jax.random.normal(arg_keys[4], (D,), jnp.float32), 0.25, 1.75)
    space_qkv = draw_space_qkv(jax.random.fold_in(arg_keys[10], 71), 0)
    space_out = centred(arg_keys[6], (HEADS * HEAD_DIM, D), (HEADS * HEAD_DIM) ** -0.5, 0.125, ((0, 8),))
    time_gain = jnp.clip(1.0 + 0.15 * jax.random.normal(arg_keys[7], (D,), jnp.float32), 0.25, 1.75)
    time_qkv = draw_time_qkv(jax.random.fold_in(arg_keys[10], 71), 0)
    time_out = centred(arg_keys[9], (HEADS * HEAD_DIM, D), (HEADS * HEAD_DIM) ** -0.5, 0.125, ((0, 8),))
    return dict(tokens=tokens, action_rows=action_rows, pair_index=pair_index, episode_id=episode_id, space_gain=space_gain, space_qkv=space_qkv, space_out=space_out, time_gain=time_gain, time_qkv=time_qkv, time_out=time_out)


EPSILON = 1e-06

def root_norm(values, gain):
    return values * lax.rsqrt(lax.optimization_barrier(jnp.mean(values * values, -1, keepdims=True)) + EPSILON) * gain

def reference(tokens, action_rows, pair_index, episode_id, space_gain, space_qkv, space_out, time_gain, time_qkv, time_out):
    frame_count = tokens.shape[0]
    picker = (pair_index[:, None] == jnp.arange(frame_count, dtype=jnp.int32)[None, :]).astype(jnp.bfloat16)
    action = jnp.dot(picker, action_rows, preferred_element_type=jnp.float32)
    start = tokens.astype(jnp.float32) + action[:, None, :]
    space_normed = root_norm(start, space_gain).astype(jnp.bfloat16)

    def space_frame(frame_rows):
        query = jnp.dot(frame_rows, space_qkv[0], preferred_element_type=jnp.float32).astype(jnp.bfloat16)
        keys = jnp.dot(frame_rows, space_qkv[1], preferred_element_type=jnp.float32).astype(jnp.bfloat16)
        values = jnp.dot(frame_rows, space_qkv[2], preferred_element_type=jnp.float32).astype(jnp.bfloat16)
        query = query.reshape(FRAME_TOKENS, HEADS, HEAD_DIM).astype(jnp.float32)
        keys = keys.reshape(FRAME_TOKENS, HEADS, HEAD_DIM).astype(jnp.float32)
        values = values.reshape(FRAME_TOKENS, HEADS, HEAD_DIM).astype(jnp.float32)
        scores = jnp.einsum('qhd,khd->hqk', query, keys) * HEAD_DIM ** (-0.5)
        probabilities = jax.nn.softmax(scores, -1).astype(jnp.bfloat16).astype(jnp.float32)
        mixture = jnp.einsum('hqk,khd->qhd', probabilities, values).astype(jnp.bfloat16)
        return jnp.dot(mixture.reshape(FRAME_TOKENS, HEADS * HEAD_DIM), space_out, preferred_element_type=jnp.float32)
    middle = start + lax.map(space_frame, space_normed)
    time_normed = root_norm(middle, time_gain).astype(jnp.bfloat16).reshape(frame_count * FRAME_TOKENS, D)
    projected = []
    for index in range(3):
        piece_out = jnp.dot(time_normed, time_qkv[index], preferred_element_type=jnp.float32).astype(jnp.bfloat16)
        projected.append(piece_out.reshape(frame_count, FRAME_TOKENS, HEADS, HEAD_DIM).astype(jnp.float32))
    scores = jnp.einsum('fphd,gphd->phfg', projected[0], projected[1]) * HEAD_DIM ** (-0.5)
    order = jnp.arange(frame_count, dtype=jnp.int32)
    allowed = (episode_id[:, None] == episode_id[None, :]) & (order[None, :] <= order[:, None])
    scores = jnp.where(allowed, scores, -1e+30)
    probabilities = jax.nn.softmax(scores, -1).astype(jnp.bfloat16).astype(jnp.float32)
    mixture = jnp.einsum('phfg,gphd->fphd', probabilities, projected[2]).astype(jnp.bfloat16)
    update = jnp.dot(mixture.reshape(frame_count * FRAME_TOKENS, HEADS * HEAD_DIM), time_out, preferred_element_type=jnp.float32)
    return (middle + update.reshape(frame_count, FRAME_TOKENS, D)).astype(jnp.bfloat16)
```

```python
import jax
import jax.numpy as jnp
from jax import lax
from jax.experimental import pallas as pl
from jax.experimental.pallas import tpu as pltpu
from jax.sharding import PartitionSpec as P

MESH = pl.DeviceIdType.MESH
HEAD_DIM = 128
EPSILON = 1e-06
SCALE = HEAD_DIM ** (-0.5)
TM, Z = 32, 8
CHUNKS, ROWS, COLS, WIDTH = 3, 256, 256, 2048
TOKENS = CHUNKS * ROWS
PLACES = ROWS // TM
BF, F32 = jnp.bfloat16, jnp.float32


def kernel(
    tokens, action, pair, episode, space_gain, space_qkv, space_out, time_gain, time_qkv, time_out,
    out,
    tokf, af, tfb, wq, wt, wo, to, arow, act, actz, row, xn, mid, midz, qkv, mask, snd, rcv, snd2, rcv2,
    ag_send, ag_recv, w_send, w_recv, loc, one_send, one_recv, a2a_send, a2a_recv,
):
    tm, z = lax.axis_index("tm"), lax.axis_index("tensor")
    y, x, k = tm // 8, lax.rem(tm // 2, 4), lax.rem(tm, 2)
    chip = tm // 2
    zr, zl = lax.rem(z + 1, Z), lax.rem(z + Z - 1, Z)

    def remote(src, dst, ssem, rsem, t, zz):
        return pltpu.make_async_remote_copy(
            src_ref=src, dst_ref=dst, send_sem=ssem, recv_sem=rsem, device_id=(t, zz), device_id_type=MESH
        )

    def bulk(ref, sem):
        pltpu.make_async_copy(ref, ref, sem).wait()

    def each(n, me, fn):
        def step(j, carry):
            fn(lax.rem(me + j, n))
            return carry
        lax.fori_loop(1, n, step, 0)

    own = pl.multiple_of(z * COLS, COLS)

    load_wq = pltpu.make_async_copy(space_qkv, wq, loc.at[0])
    load_wt = pltpu.make_async_copy(time_qkv, wt, loc.at[1])
    load_wq.start()
    load_wt.start()
    load_tok = pltpu.make_async_copy(tokens.at[0], tokf.at[:, pl.ds(own, COLS)], loc.at[2])
    load_tok.start()
    arow[...] = jnp.broadcast_to(action[...].astype(F32), (8, COLS)).astype(BF)

    barrier = pltpu.get_barrier_semaphore()
    each(TM, tm, lambda t: pl.semaphore_signal(barrier, inc=1, device_id=(t, z), device_id_type=MESH))
    each(Z, z, lambda q: pl.semaphore_signal(barrier, inc=1, device_id=(tm, q), device_id_type=MESH))
    pl.semaphore_wait(barrier, TM - 1 + Z - 1)

    def gather(n, view, half, first):
        def copy(d, s, i):
            origin = lax.rem(z + (Z - s if d == 0 else s), Z)
            if s == 3:
                src = dst = half(i, origin, d)
            else:
                dst = view(i, origin)
                src = first(i) if s == 0 else dst
            return remote(src, dst, ag_send.at[n, d, s, i], ag_recv.at[n, d, s, i], tm, zr if d == 0 else zl)

        def send(s, i):
            for d in (0, 1):
                if s:
                    copy(d, s - 1, i).wait_recv()
                copy(d, s, i).start()

        def finish(i):
            for d in (0, 1):
                copy(d, 3, i).wait_recv()

        def drain():
            for d in (0, 1):
                for s in range(4):
                    for i in range(CHUNKS):
                        copy(d, s, i).wait_send()

        return send, finish, drain

    def flat(buf):
        def view(i, origin):
            return buf.at[pl.ds(ROWS * i, ROWS), pl.ds(pl.multiple_of(origin * COLS, COLS), COLS)]

        def half(i, origin, d):
            return buf.at[
                pl.ds(ROWS * i + d * (ROWS // 2), ROWS // 2), pl.ds(pl.multiple_of(origin * COLS, COLS), COLS)
            ]
        return view, half

    tok_view, tok_half = flat(tokf)
    tok_send, tok_finish, tok_drain = gather(
        0, tok_view, tok_half, lambda i: tokens.at[0, pl.ds(ROWS * i, ROWS), :]
    )
    a_view, a_half = flat(af)
    a_send, a_finish, a_drain = gather(1, a_view, a_half, lambda i: a_view(i, z))
    t_send, t_finish, t_drain = gather(
        2,
        lambda i, origin: tfb.at[origin, i],
        lambda i, origin, d: tfb.at[origin, i, pl.ds(d * (TM // 2), TM // 2)],
        lambda i: rcv2.at[i],
    )

    p, r = y + k * (x - y), x + k * (y - x)

    def place(pp, rr):
        return ((pp * 4 + rr) * (1 - k) + (rr * 4 + pp) * k) * 2 + k

    p1, p3, p2 = lax.rem(p + 1, 4), lax.rem(p + 3, 4), lax.rem(p + 2, 4)
    r1, r3 = lax.rem(r + 1, 4), lax.rem(r + 3, 4)
    w_src = space_out.at[pl.ds(pl.multiple_of(k * 128, 128), 128), pl.ds(pl.multiple_of(chip * 128, 128), 128)]

    def w0(q):
        return remote(w_src, wo.at[k, p, r, z], one_send.at[0], one_recv.at[0], tm, q)

    def w0_local():
        return pltpu.make_async_copy(w_src, wo.at[k, p, r, z], one_recv.at[0])

    def w1(d):
        return remote(wo.at[k, p, r], wo.at[k, p, r], w_send.at[d], w_recv.at[d], place(p, r1 if d == 0 else r3), z)

    def w1b(d):
        ref = wo.at[k, p, r3 if d == 0 else r1, pl.ds(4 * d, 4)]
        return remote(ref, ref, w_send.at[2 + d], w_recv.at[2 + d], place(p, r1 if d == 0 else r3), z)

    def w2(d):
        return remote(wo.at[k, p], wo.at[k, p], w_send.at[4 + d], w_recv.at[4 + d], place(p1 if d == 0 else p3, r), z)

    def w2b(d):
        ref = wo.at[k, p3 if d == 0 else p1, pl.ds(2 * d, 2)]
        return remote(ref, ref, w_send.at[6 + d], w_recv.at[6 + d], place(p1 if d == 0 else p3, r), z)

    def w3(n):
        ref = wo.at[k, (p, p1, p3, p2)[n]]
        return remote(ref, ref, w_send.at[8 + n], w_recv.at[8 + n], tm + 1 - 2 * k, z)

    def t_src(q):
        return time_out.at[
            pl.ds(pl.multiple_of(chip * 16, 16), 16), pl.ds(pl.multiple_of(q * COLS, COLS), COLS)
        ]

    def t0(q):
        return remote(t_src(q), to.at[z, chip], one_send.at[1], one_recv.at[1], tm, q)

    def t0_local():
        return pltpu.make_async_copy(t_src(z), to.at[z, chip], one_recv.at[1])

    def t1(c):
        return remote(to.at[:, chip], to.at[:, chip], one_send.at[2], one_recv.at[2], c * 2 + k, z)

    def act_copy(t):
        return remote(arow, act.at[tm], one_send.at[3], one_recv.at[3], t, z)

    def actz_copy(q):
        return remote(actz.at[z], actz.at[z], one_send.at[4], one_recv.at[4], tm, q)

    each(Z, z, lambda q: w0(q).start())
    w0_local().start()
    each(TM, tm, lambda t: act_copy(t).start())
    act_local = pltpu.make_async_copy(arow, act.at[tm], one_recv.at[3])
    act_local.start()
    for i in range(CHUNKS):
        tok_send(0, i)

    one = lax.broadcasted_iota(jnp.int32, (ROWS, 128), 0)
    two = lax.broadcasted_iota(jnp.int32, (8, ROWS), 1)
    one_f, two_f = lax.shift_right_logical(one, 3), lax.shift_right_logical(two, 3)
    one_e, two_e = jnp.zeros_like(one), jnp.zeros_like(two)
    for f in range(TM):
        one_e = jnp.where(one_f == f, episode[f], one_e)
        two_e = jnp.where(two_f == f, episode[f], two_e)

    def wide_row(v):
        return jnp.concatenate([v, v], axis=1)

    def wide_col(v):
        return jnp.broadcast_to(v[0:1], (ROWS, ROWS))

    allowed = (
        (wide_row(one_e) == wide_col(two_e))
        & (wide_col(two_f) <= wide_row(one_f))
        & (wide_row(one & 7) == wide_col(two & 7))
    )
    mask[...] = jnp.where(allowed, 1.0, 0.0)

    bulk(act, one_recv.at[3])
    actz[z] = act[pair[0]]
    each(Z, z, lambda q: actz_copy(q).start())

    for i in range(CHUNKS):
        tok_send(1, i)
    bulk(wo.at[k, p, r], one_recv.at[0])
    w1(0).start()
    w1(1).start()
    tok_send(2, 0)
    tok_send(2, 1)
    for d in (0, 1):
        w1(d).wait_recv()
        w1b(d).start()
    tok_send(2, 2)
    for d in (0, 1):
        w1b(d).wait_recv()
    w2(0).start()
    w2(1).start()
    w3(0).start()
    load_wq.wait()
    load_tok.wait()
    bulk(actz.at[pl.ds(0, Z - 1)], one_recv.at[4])
    for q in range(Z):
        row[:, COLS * q : COLS * (q + 1)] = actz[q].astype(F32)
    for i in range(CHUNKS):
        tok_send(3, i)
    each(Z, z, lambda q: t0(q).start())
    t0_local().start()

    STEP = 32

    def normed(get, gain):
        def tile(n, carry):
            at = pl.multiple_of(n * STEP, STEP)
            v = get(at)
            factor = lax.rsqrt(jnp.sum(v * v, -1, keepdims=True) * (1.0 / WIDTH) + EPSILON)
            xn[pl.ds(at, STEP), :] = (v * factor * gain[...]).astype(BF)
            return carry
        lax.fori_loop(0, ROWS // STEP, tile, 0)

    for i in range(CHUNKS):
        tok_finish(i)

        def start_tile(at, i=i):
            return tokf[pl.ds(ROWS * i + at, STEP), :].astype(F32) + row[0:1, :]

        normed(start_tile, space_gain)
        for n in range(3):
            qkv[n, ROWS * i : ROWS * (i + 1), :] = jnp.dot(xn[...], wq[n], preferred_element_type=F32).astype(BF)
        if i == 0:
            for d in (0, 1):
                w2(d).wait_recv()
                w2b(d).start()
            w3(1).start()
            w3(2).start()
            bulk(to.at[:, 0], one_recv.at[1])
            each(TM // 2, chip, lambda c: t1(c).start())

    def attend(i):
        for h in range(2):
            cols = slice(HEAD_DIM * h, HEAD_DIM * (h + 1))
            s = lax.dot_general(
                qkv[0, ROWS * i : ROWS * (i + 1), cols], qkv[1, :, cols], (((1,), (1,)), ((), ())),
                preferred_element_type=F32,
            ) * SCALE
            e = jnp.exp(s - jnp.max(s, -1, keepdims=True))
            prob = (e / jnp.sum(e, -1, keepdims=True)).astype(BF)
            o = jnp.dot(prob, qkv[2, :, cols], preferred_element_type=F32)
            at = pl.multiple_of(z * COLS + HEAD_DIM * h, HEAD_DIM)
            af[ROWS * i : ROWS * (i + 1), pl.ds(at, HEAD_DIM)] = o.astype(BF)

    def project(i, lo, hi):
        rows = slice(ROWS * i, ROWS * (i + 1))

        def tile(j, carry):
            yy, xx = j // 2, 2 * lax.rem(j, 2)

            def rhs(kk):
                a, b = ((yy, xx), (yy, xx + 1)) if kk == 0 else ((xx, yy), (xx + 1, yy))
                return jnp.concatenate(
                    [wo[kk, a[0], a[1]].reshape(1024, 128), wo[kk, b[0], b[1]].reshape(1024, 128)], axis=1
                )

            def lhs(kk):
                return jnp.concatenate(
                    [af[rows, COLS * q + 128 * kk : COLS * q + 128 * (kk + 1)] for q in range(Z)], axis=1
                )

            at = pl.multiple_of(j * COLS, COLS)
            total = jnp.dot(lhs(0), rhs(0), preferred_element_type=F32)
            total = total + jnp.dot(lhs(1), rhs(1), preferred_element_type=F32)
            start = tokf[rows, pl.ds(at, COLS)].astype(F32) + row[0:1, pl.ds(at, COLS)]
            mid[:, pl.ds(at, COLS)] = start + total
            return carry
        lax.fori_loop(lo, hi, tile, 0)

    def renorm(i):
        normed(lambda at: mid[pl.ds(at, STEP), :], time_gain)
        midz[ROWS * i : ROWS * (i + 1), :] = mid[:, pl.ds(own, COLS)]

    def qkv_copy(i, t):
        return remote(snd.at[i, t], rcv.at[i, tm], a2a_send.at[0, i], a2a_recv.at[0, i], t, z)

    def scatter(i):
        for n in range(3):
            v = jnp.dot(xn[...], wt[n], preferred_element_type=F32)
            snd[i, :, :, COLS * n : COLS * (n + 1)] = v.reshape(TM, PLACES, COLS).astype(BF)
        each(TM, tm, lambda t: qkv_copy(i, t).start())
        pltpu.make_async_copy(snd.at[i, tm], rcv.at[i, tm], a2a_recv.at[0, i]).start()

    def mix_copy(i, t):
        return remote(snd2.at[i, t], rcv2.at[i, tm], a2a_send.at[1, i], a2a_recv.at[1, i], t, z)

    def mix(i):
        bulk(rcv.at[i], a2a_recv.at[0, i])

        def take(n, h):
            at = COLS * n + HEAD_DIM * h
            return rcv[i, :, :, at : at + HEAD_DIM].astype(F32).reshape(ROWS, HEAD_DIM).astype(BF)

        for h in range(2):
            s = lax.dot_general(
                take(0, h), take(1, h), (((1,), (1,)), ((), ())), preferred_element_type=F32
            ) * SCALE
            s = jnp.where(mask[...] > 0.5, s, -1e30)
            e = jnp.exp(s - jnp.max(s, -1, keepdims=True))
            prob = (e / jnp.sum(e, -1, keepdims=True)).astype(BF)
            o = jnp.dot(prob, take(2, h), preferred_element_type=F32)
            snd2[i, :, :, HEAD_DIM * h : HEAD_DIM * (h + 1)] = o.reshape(TM, PLACES, HEAD_DIM).astype(BF)
        each(TM, tm, lambda t: mix_copy(i, t).start())
        pltpu.make_async_copy(snd2.at[i, tm], rcv2.at[i, tm], a2a_recv.at[1, i]).start()

    def back(i):
        bulk(rcv2.at[i], a2a_recv.at[1, i])
        t_send(0, i)
        pltpu.make_async_copy(rcv2.at[i], tfb.at[z, i], loc.at[3 + i]).start()

    def finish(i):
        t_finish(i)
        pltpu.make_async_copy(rcv2.at[i], tfb.at[z, i], loc.at[3 + i]).wait()
        lhs = jnp.concatenate([tfb[q, i].astype(F32).reshape(ROWS, COLS).astype(BF) for q in range(Z)], axis=1)
        update = jnp.dot(lhs, to[...].reshape(WIDTH, COLS), preferred_element_type=F32)
        rows = slice(ROWS * i, ROWS * (i + 1))
        out[0, rows, :] = (midz[rows, :] + update).astype(BF)

    attend(0)
    a_send(0, 0)
    attend(1)
    a_send(0, 1)
    a_send(1, 0)
    for d in (0, 1):
        w2b(d).wait_recv()
    w3(3).start()
    attend(2)
    a_send(0, 2)
    a_send(2, 0)
    a_send(1, 1)
    a_send(3, 0)
    a_send(1, 2)
    a_send(2, 1)
    load_wt.wait()
    for n in range(4):
        w3(n).wait_recv()
    a_finish(0)
    project(0, 0, 4)
    project(0, 4, 8)
    a_send(2, 2)
    a_send(3, 1)
    renorm(0)
    scatter(0)
    a_send(3, 2)
    a_finish(1)
    project(1, 0, 8)
    mix(0)
    renorm(1)
    scatter(1)
    back(0)
    a_finish(2)
    project(2, 0, 4)
    mix(1)
    project(2, 4, 8)
    t_send(1, 0)
    renorm(2)
    back(1)
    scatter(2)
    t_send(2, 0)
    t_send(1, 1)
    t_send(3, 0)
    mix(2)
    t_send(2, 1)
    back(2)
    t_send(3, 1)
    bulk(to.at[:, pl.ds(0, TM // 2 - 1)], one_recv.at[2])
    finish(0)
    t_send(1, 2)
    t_send(2, 2)
    finish(1)
    t_send(3, 2)
    finish(2)

    tok_drain()
    a_drain()
    t_drain()
    bulk(wo.at[0, 0, 0, pl.ds(0, Z - 1)], one_send.at[0])
    bulk(to.at[pl.ds(0, Z - 1), 0], one_send.at[1])
    bulk(to.at[:, pl.ds(0, TM // 2 - 1)], one_send.at[2])
    bulk(act.at[pl.ds(0, TM - 1)], one_send.at[3])
    bulk(actz.at[pl.ds(0, Z - 1)], one_send.at[4])
    for d in (0, 1):
        w1(d).wait_send()
        w1b(d).wait_send()
        w2(d).wait_send()
        w2b(d).wait_send()
    for n in range(4):
        w3(n).wait_send()
    for i in range(CHUNKS):
        bulk(snd.at[i, pl.ds(0, TM - 1)], a2a_send.at[0, i])
        bulk(snd2.at[i, pl.ds(0, TM - 1)], a2a_send.at[1, i])


def body(
    tokens, action_rows, pair_index, episode_id, space_gain, space_qkv, space_out, time_gain, time_qkv, time_out
):
    any_, vmem, smem = (pl.BlockSpec(memory_space=m) for m in (pl.ANY, pltpu.VMEM, pltpu.SMEM))
    dma = pltpu.SemaphoreType.DMA
    return pl.pallas_call(
        kernel,
        out_shape=jax.ShapeDtypeStruct(tokens.shape, BF),
        in_specs=[any_, vmem, smem, smem, vmem, any_, any_, vmem, any_, any_],
        out_specs=vmem,
        scratch_shapes=[
            pltpu.VMEM((TOKENS, WIDTH), BF),
            pltpu.VMEM((TOKENS, WIDTH), BF),
            pltpu.VMEM((Z, CHUNKS, TM, PLACES, COLS), BF),
            pltpu.VMEM((3, WIDTH, COLS), BF),
            pltpu.VMEM((3, WIDTH, COLS), BF),
            pltpu.VMEM((2, 4, 4, Z, 128, 128), BF),
            pltpu.VMEM((Z, TM // 2, 16, COLS), BF),
            pltpu.VMEM((8, COLS), BF),
            pltpu.VMEM((TM, 8, COLS), BF),
            pltpu.VMEM((Z, 8, COLS), BF),
            pltpu.VMEM((8, WIDTH), F32),
            pltpu.VMEM((ROWS, WIDTH), BF),
            pltpu.VMEM((ROWS, WIDTH), F32),
            pltpu.VMEM((TOKENS, COLS), F32),
            pltpu.VMEM((3, TOKENS, COLS), BF),
            pltpu.VMEM((ROWS, ROWS), F32),
            pltpu.VMEM((CHUNKS, TM, PLACES, 3 * COLS), BF),
            pltpu.VMEM((CHUNKS, TM, PLACES, 3 * COLS), BF),
            pltpu.VMEM((CHUNKS, TM, PLACES, COLS), BF),
            pltpu.VMEM((CHUNKS, TM, PLACES, COLS), BF),
            dma((3, 2, 4, CHUNKS)),
            dma((3, 2, 4, CHUNKS)),
            dma((12,)),
            dma((12,)),
            dma((6,)),
            dma((5,)),
            dma((5,)),
            dma((2, CHUNKS)),
            dma((2, CHUNKS)),
        ],
        compiler_params=pltpu.CompilerParams(
            collective_id=0, has_side_effects=True, vmem_limit_bytes=60 * 1024 * 1024
        ),
    )(
        tokens, action_rows, pair_index, episode_id, space_gain.reshape(1, WIDTH), space_qkv, space_out,
        time_gain.reshape(1, WIDTH), time_qkv, time_out,
    )


def solution(mesh):
    return jax.shard_map(
        body,
        mesh=mesh,
        in_specs=(
            P("tm", None, "tensor"),
            P("tm", "tensor"),
            P("tm"),
            P(),
            P(),
            P(None, None, "tensor"),
            P("tensor", None),
            P(),
            P(None, None, "tensor"),
            P("tensor", None),
        ),
        out_specs=P("tm", None, "tensor"),
        check_vma=False,
    )
```

```python
import jax
import jax.numpy as jnp
from jax import lax
from jax.experimental import pallas as pl
from jax.experimental.pallas import tpu as pltpu
from jax.sharding import PartitionSpec as P

MESH = pl.DeviceIdType.MESH
HEAD_DIM = 128
EPSILON = 1e-06
SCALE = HEAD_DIM ** (-0.5)
TM, Z = 32, 8
CHUNKS, ROWS, COLS, WIDTH = 3, 256, 256, 2048
TOKENS = CHUNKS * ROWS
PLACES = ROWS // TM
BF, F32 = jnp.bfloat16, jnp.float32
ORDER = [
    ("w0", 0), ("act",), ("t0",), ("w0", 1), ("k", 0, 0, 0), ("mask",), ("k", 0, 0, 1), ("k", 0, 1, 0),
    ("k", 0, 1, 1), ("w0", 2), ("sel",), ("t1",), ("k", 1, 0, 0), ("k", 1, 0, 1), ("k", 1, 1, 0), ("k", 1, 1, 1),
    ("w0", 3), ("k", 2, 0, 0), ("k", 2, 0, 1), ("k", 2, 1, 0), ("k", 2, 1, 1), ("w1",), ("wp", 0), ("k", 0, 2, 0),
    ("k", 3, 0, 0), ("k", 3, 0, 1), ("k", 0, 2, 1), ("k", 3, 1, 0), ("k", 3, 1, 1), ("w1b",), ("wp", 1), ("wp", 2),
    ("k", 1, 2, 0), ("q", 0), ("k", 1, 2, 1), ("wpb", 0), ("q", 1), ("wp", 3), ("k", 2, 2, 0), ("k", 2, 2, 1),
    ("k", 3, 2, 0), ("wpb", 1), ("k", 3, 2, 1), ("q", 2), ("wpb", 2), ("att", 0), ("a", 0, 0, 0), ("a", 0, 0, 1),
    ("w3", 0), ("att", 1), ("a", 0, 1, 0), ("att", 2), ("a", 0, 1, 1), ("a", 1, 0, 0), ("wpb", 3), ("a", 1, 0, 1),
    ("w3", 1), ("a", 1, 1, 0), ("a", 1, 1, 1), ("w3", 2), ("a", 2, 0, 0), ("w3", 3), ("a", 2, 0, 1), ("a", 2, 1, 0),
    ("a", 2, 1, 1), ("a", 3, 0, 0), ("a", 3, 0, 1), ("a", 0, 2, 0), ("a", 3, 1, 0), ("a", 3, 1, 1), ("a", 0, 2, 1),
    ("p", 0, 0), ("p", 0, 1), ("a", 1, 2, 0), ("p", 0, 2), ("p", 0, 3), ("r", 0), ("a", 1, 2, 1), ("s", 0),
    ("a", 2, 2, 0), ("p", 1, 0), ("p", 1, 1), ("a", 2, 2, 1), ("p", 1, 2), ("p", 1, 3), ("a", 3, 2, 0), ("r", 1),
    ("a", 3, 2, 1), ("s", 1), ("p", 2, 0), ("p", 2, 1), ("m", 0), ("p", 2, 2), ("p", 2, 3), ("r", 2), ("s", 2),
    ("m", 1), ("t", 0, 0, 0), ("t", 0, 0, 1), ("t", 1, 0, 0), ("t", 1, 0, 1), ("t", 2, 0, 0), ("m", 2),
    ("t", 2, 0, 1), ("t", 0, 1, 0), ("t", 3, 0, 0), ("t", 0, 1, 1), ("t", 3, 0, 1), ("t", 1, 1, 0), ("t", 0, 2, 0),
    ("t", 1, 1, 1), ("f", 0), ("t", 0, 2, 1), ("t", 2, 1, 0), ("t", 1, 2, 0), ("t", 2, 1, 1), ("t", 1, 2, 1),
    ("t", 3, 1, 0), ("t", 2, 2, 0), ("t", 3, 1, 1), ("t", 2, 2, 1), ("t", 3, 2, 0), ("f", 1), ("t", 3, 2, 1),
    ("f", 2),
]


def kernel(
    tokens, action, pair, episode, space_gain, space_qkv, space_out, time_gain, time_qkv, time_out,
    out,
    tokf, af, tfb, wq, wt, wo, to, arow, act, actz, row, xn, mid, midz, qkv, mask, snd, rcv, snd2, rcv2,
    tok_ss, tok_rs, a_ss, a_rs, t_ss, t_rs, w0_ss, w0_rs, w_send, w_recv, loc, one_send, one_recv, a2a_send, a2a_recv,
):
    tm, z = lax.axis_index("tm"), lax.axis_index("tensor")
    y, x, k = tm // 8, lax.rem(tm // 2, 4), lax.rem(tm, 2)
    chip = tm // 2
    zr, zl = lax.rem(z + 1, Z), lax.rem(z + Z - 1, Z)

    def remote(src, dst, ssem, rsem, t, zz):
        return pltpu.make_async_remote_copy(
            src_ref=src, dst_ref=dst, send_sem=ssem, recv_sem=rsem, device_id=(t, zz), device_id_type=MESH
        )

    def bulk(ref, sem):
        pltpu.make_async_copy(ref, ref, sem).wait()

    def each(n, me, fn):
        def step(j, carry):
            fn(lax.rem(me + j, n))
            return carry
        lax.fori_loop(1, n, step, 0)

    own = pl.multiple_of(z * COLS, COLS)

    load_wq = pltpu.make_async_copy(space_qkv, wq, loc.at[0])
    load_wt = pltpu.make_async_copy(time_qkv, wt, loc.at[1])
    load_wq.start()
    load_wt.start()
    load_tok = pltpu.make_async_copy(tokens.at[0], tokf.at[:, pl.ds(own, COLS)], loc.at[2])
    load_tok.start()
    arow[...] = jnp.broadcast_to(action[...].astype(F32), (8, COLS)).astype(BF)

    barrier = pltpu.get_barrier_semaphore()
    each(TM, tm, lambda t: pl.semaphore_signal(barrier, inc=1, device_id=(t, z), device_id_type=MESH))
    each(Z, z, lambda q: pl.semaphore_signal(barrier, inc=1, device_id=(tm, q), device_id_type=MESH))
    pl.semaphore_wait(barrier, TM - 1 + Z - 1)

    seen = set()

    def once(key, wait):
        if key not in seen:
            seen.add(key)
            wait()

    def gather(name, view, first, ssem, rsem, chunks):
        def copy(d, s, i, h):
            origin = lax.rem(z + (Z - s if d == 0 else s), Z)
            dst = view(i, h, origin)
            src = first(i, h) if s == 0 else dst
            return remote(src, dst, ssem.at[d, s, i, h], rsem.at[d, s, i, h], tm, zr if d == 0 else zl)

        def arrived(d, s, i, h):
            once((name, d, s, i, h), lambda: copy(d, s, i, h).wait_recv())

        def send(s, i, h):
            for d in (0, 1):
                if s < 3 or h == d:
                    if s:
                        arrived(d, s - 1, i, h)
                    copy(d, s, i, h).start()

        def finish(i):
            for d in (0, 1):
                for s in range(4):
                    for h in (0, 1):
                        if s < 3 or h == d:
                            arrived(d, s, i, h)

        def drain():
            for i in range(chunks):
                for d in (0, 1):
                    for s in range(4):
                        for h in (0, 1):
                            if s < 3 or h == d:
                                copy(d, s, i, h).wait_send()

        return send, finish, drain

    HALF = ROWS // 2

    def flat(buf):
        def view(i, h, origin):
            return buf.at[
                pl.ds(ROWS * i + HALF * h, HALF), pl.ds(pl.multiple_of(origin * COLS, COLS), COLS)
            ]
        return view

    tok_send, tok_finish, tok_drain = gather(
        0, flat(tokf), lambda i, h: tokens.at[0, pl.ds(ROWS * i + HALF * h, HALF), :], tok_ss, tok_rs, CHUNKS
    )
    a_view = flat(af)
    a_send, a_finish, a_drain = gather(1, a_view, lambda i, h: a_view(i, h, z), a_ss, a_rs, CHUNKS)
    t_send, t_finish, t_drain = gather(
        2, lambda i, h, origin: tfb.at[origin, i, pl.ds(h * (TM // 2), TM // 2)],
        lambda i, h: rcv2.at[i, pl.ds(h * (TM // 2), TM // 2)],
        t_ss, t_rs, CHUNKS,
    )

    p, r = y + k * (x - y), x + k * (y - x)

    def place(pp, rr):
        return ((pp * 4 + rr) * (1 - k) + (rr * 4 + pp) * k) * 2 + k

    p1, p3 = lax.rem(p + 1, 4), lax.rem(p + 3, 4)
    r1, r3, r2 = lax.rem(r + 1, 4), lax.rem(r + 3, 4), lax.rem(r + 2, 4)
    w_src = space_out.at[pl.ds(pl.multiple_of(k * 128, 128), 128), pl.ds(pl.multiple_of(chip * 128, 128), 128)]

    w0_send, w0_finish, w0_drain = gather(
        3, lambda i, h, origin: wo.at[k, p, r, origin, pl.ds(64 * h, 64)],
        lambda i, h: space_out.at[
            pl.ds(pl.multiple_of(k * 128 + 64 * h, 64), 64), pl.ds(pl.multiple_of(chip * 128, 128), 128)
        ],
        w0_ss, w0_rs, 1,
    )
    w0_local = pltpu.make_async_copy(w_src, wo.at[k, p, r, z], loc.at[6])

    def w1(d):
        return remote(wo.at[k, p, r], wo.at[k, p, r], w_send.at[d], w_recv.at[d], place(p, r1 if d == 0 else r3), z)

    def w1b(d):
        ref = wo.at[k, p, r3 if d == 0 else r1, pl.ds(4 * d, 4)]
        return remote(ref, ref, w_send.at[2 + d], w_recv.at[2 + d], place(p, r1 if d == 0 else r3), z)

    def wp(e, d):
        ref = wo.at[k, p, (r, r3, r1, r2)[e]]
        n = 4 + 2 * e + d
        return remote(ref, ref, w_send.at[n], w_recv.at[n], place(p1 if d == 0 else p3, r), z)

    def wpb(e, d):
        ref = wo.at[k, p3 if d == 0 else p1, (r, r3, r1, r2)[e], pl.ds(4 * d, 4)]
        n = 12 + 2 * e + d
        return remote(ref, ref, w_send.at[n], w_recv.at[n], place(p1 if d == 0 else p3, r), z)

    def w3(e):
        ref = wo.at[k, :, (r, r3, r1, r2)[e]]
        return remote(ref, ref, w_send.at[20 + e], w_recv.at[20 + e], tm + 1 - 2 * k, z)

    def w_arrived(name, fn, *at):
        once((name, at), lambda: fn(*at).wait_recv())

    def t_src(q):
        return time_out.at[
            pl.ds(pl.multiple_of(chip * 16, 16), 16), pl.ds(pl.multiple_of(q * COLS, COLS), COLS)
        ]

    def t0(q):
        return remote(t_src(q), to.at[z, chip], one_send.at[1], one_recv.at[1], tm, q)

    def t0_local():
        return pltpu.make_async_copy(t_src(z), to.at[z, chip], one_recv.at[1])

    def t1(c):
        return remote(to.at[:, chip], to.at[:, chip], one_send.at[2], one_recv.at[2], c * 2 + k, z)

    def act_copy(t):
        return remote(arow, act.at[tm], one_send.at[3], one_recv.at[3], t, z)

    def actz_copy(q):
        return remote(actz.at[z], actz.at[z], one_send.at[4], one_recv.at[4], tm, q)

    def build_mask():
        one = lax.broadcasted_iota(jnp.int32, (ROWS, 128), 0)
        two = lax.broadcasted_iota(jnp.int32, (8, ROWS), 1)
        one_f, two_f = lax.shift_right_logical(one, 3), lax.shift_right_logical(two, 3)
        one_e, two_e = jnp.zeros_like(one), jnp.zeros_like(two)
        for f in range(TM):
            one_e = jnp.where(one_f == f, episode[f], one_e)
            two_e = jnp.where(two_f == f, episode[f], two_e)

        def wide_row(v):
            return jnp.concatenate([v, v], axis=1)

        def wide_col(v):
            return jnp.broadcast_to(v[0:1], (ROWS, ROWS))

        allowed = (
            (wide_row(one_e) == wide_col(two_e))
            & (wide_col(two_f) <= wide_row(one_f))
            & (wide_row(one & 7) == wide_col(two & 7))
        )
        mask[...] = jnp.where(allowed, 1.0, 0.0)

    STEP = 32

    def normed(get, gain):
        def tile(n, carry):
            at = pl.multiple_of(n * STEP, STEP)
            v = get(at)
            factor = lax.rsqrt(jnp.sum(v * v, -1, keepdims=True) * (1.0 / WIDTH) + EPSILON)
            xn[pl.ds(at, STEP), :] = (v * factor * gain[...]).astype(BF)
            return carry
        lax.fori_loop(0, ROWS // STEP, tile, 0)

    def spatial(i):
        if i == 0:
            load_wq.wait()
            load_tok.wait()
            bulk(actz.at[pl.ds(0, Z - 1)], one_recv.at[4])
            for q in range(Z):
                row[:, COLS * q : COLS * (q + 1)] = actz[q].astype(F32)
        tok_finish(i)

        def start_tile(at):
            return tokf[pl.ds(ROWS * i + at, STEP), :].astype(F32) + row[0:1, :]

        normed(start_tile, space_gain)
        for n in range(3):
            qkv[n, ROWS * i : ROWS * (i + 1), :] = jnp.dot(xn[...], wq[n], preferred_element_type=F32).astype(BF)

    def attend(i):
        for h in range(2):
            cols = slice(HEAD_DIM * h, HEAD_DIM * (h + 1))
            s = lax.dot_general(
                qkv[0, ROWS * i : ROWS * (i + 1), cols], qkv[1, :, cols], (((1,), (1,)), ((), ())),
                preferred_element_type=F32,
            ) * SCALE
            e = jnp.exp(s - jnp.max(s, -1, keepdims=True))
            prob = (e / jnp.sum(e, -1, keepdims=True)).astype(BF)
            o = jnp.dot(prob, qkv[2, :, cols], preferred_element_type=F32)
            at = pl.multiple_of(z * COLS + HEAD_DIM * h, HEAD_DIM)
            af[ROWS * i : ROWS * (i + 1), pl.ds(at, HEAD_DIM)] = o.astype(BF)

    def project(i, lo, hi):
        rows = slice(ROWS * i, ROWS * (i + 1))

        def tile(j, carry):
            yy, xx = j // 2, 2 * lax.rem(j, 2)

            def rhs(kk):
                a, b = ((yy, xx), (yy, xx + 1)) if kk == 0 else ((xx, yy), (xx + 1, yy))
                return jnp.concatenate(
                    [wo[kk, a[0], a[1]].reshape(1024, 128), wo[kk, b[0], b[1]].reshape(1024, 128)], axis=1
                )

            def lhs(kk):
                return jnp.concatenate(
                    [af[rows, COLS * q + 128 * kk : COLS * q + 128 * (kk + 1)] for q in range(Z)], axis=1
                )

            at = pl.multiple_of(j * COLS, COLS)
            total = jnp.dot(lhs(0), rhs(0), preferred_element_type=F32)
            total = total + jnp.dot(lhs(1), rhs(1), preferred_element_type=F32)
            start = tokf[rows, pl.ds(at, COLS)].astype(F32) + row[0:1, pl.ds(at, COLS)]
            mid[:, pl.ds(at, COLS)] = start + total
            return carry
        lax.fori_loop(lo, hi, tile, 0)

    def renorm(i):
        normed(lambda at: mid[pl.ds(at, STEP), :], time_gain)
        midz[ROWS * i : ROWS * (i + 1), :] = mid[:, pl.ds(own, COLS)]

    def qkv_copy(i, t):
        return remote(snd.at[i, t], rcv.at[i, tm], a2a_send.at[0, i], a2a_recv.at[0, i], t, z)

    def scatter(i):
        for n in range(3):
            v = jnp.dot(xn[...], wt[n], preferred_element_type=F32)
            snd[i, :, :, COLS * n : COLS * (n + 1)] = v.reshape(TM, PLACES, COLS).astype(BF)
        each(TM, tm, lambda t: qkv_copy(i, t).start())
        pltpu.make_async_copy(snd.at[i, tm], rcv.at[i, tm], a2a_recv.at[0, i]).start()

    def mix_copy(i, t):
        return remote(snd2.at[i, t], rcv2.at[i, tm], a2a_send.at[1, i], a2a_recv.at[1, i], t, z)

    def mix(i):
        bulk(rcv.at[i], a2a_recv.at[0, i])

        def take(n, h):
            at = COLS * n + HEAD_DIM * h
            return rcv[i, :, :, at : at + HEAD_DIM].astype(F32).reshape(ROWS, HEAD_DIM).astype(BF)

        for h in range(2):
            s = lax.dot_general(
                take(0, h), take(1, h), (((1,), (1,)), ((), ())), preferred_element_type=F32
            ) * SCALE
            s = jnp.where(mask[...] > 0.5, s, -1e30)
            e = jnp.exp(s - jnp.max(s, -1, keepdims=True))
            prob = (e / jnp.sum(e, -1, keepdims=True)).astype(BF)
            o = jnp.dot(prob, take(2, h), preferred_element_type=F32)
            snd2[i, :, :, HEAD_DIM * h : HEAD_DIM * (h + 1)] = o.reshape(TM, PLACES, HEAD_DIM).astype(BF)
        each(TM, tm, lambda t: mix_copy(i, t).start())
        pltpu.make_async_copy(snd2.at[i, tm], rcv2.at[i, tm], a2a_recv.at[1, i]).start()

    def back(i):
        bulk(rcv2.at[i], a2a_recv.at[1, i])
        pltpu.make_async_copy(rcv2.at[i], tfb.at[z, i], loc.at[3 + i]).start()

    def finish(i):
        t_finish(i)
        pltpu.make_async_copy(rcv2.at[i], tfb.at[z, i], loc.at[3 + i]).wait()
        lhs = jnp.concatenate([tfb[q, i].astype(F32).reshape(ROWS, COLS).astype(BF) for q in range(Z)], axis=1)
        update = jnp.dot(lhs, to[...].reshape(WIDTH, COLS), preferred_element_type=F32)
        rows = slice(ROWS * i, ROWS * (i + 1))
        out[0, rows, :] = (midz[rows, :] + update).astype(BF)

    def act_spread():
        each(TM, tm, lambda t: act_copy(t).start())
        pltpu.make_async_copy(arow, act.at[tm], one_recv.at[3]).start()

    def act_choose():
        bulk(act, one_recv.at[3])
        actz[z] = act[pair[0]]
        each(Z, z, lambda q: actz_copy(q).start())

    def w0_step(s):
        if s == 0:
            w0_local.start()
        for h in (0, 1):
            w0_send(s, 0, h)

    def w1_step():
        w0_finish(0)
        w0_local.wait()
        w1(0).start()
        w1(1).start()

    def w1b_step():
        for d in (0, 1):
            w_arrived("w1", w1, d)
            w1b(d).start()

    def wp_step(e):
        if e in (1, 2):
            w_arrived("w1", w1, e - 1)
        if e == 3:
            w_arrived("w1b", w1b, 0)
            w_arrived("w1b", w1b, 1)
        wp(e, 0).start()
        wp(e, 1).start()

    def wpb_step(e):
        for d in (0, 1):
            w_arrived("wp", wp, e, d)
            wpb(e, d).start()

    def w3_step(e):
        for d in (0, 1):
            w_arrived("wpb", wpb, e, d)
        w3(e).start()

    def t0_step():
        each(Z, z, lambda q: t0(q).start())
        t0_local().start()

    def t1_step():
        bulk(to.at[:, 0], one_recv.at[1])
        each(TM // 2, chip, lambda c: t1(c).start())

    def p_step(i, j):
        if j == 0:
            for e in range(4):
                w_arrived("w3", w3, e)
            a_finish(i)
        project(i, 2 * j, 2 * j + 2)

    def s_step(i):
        if i == 0:
            load_wt.wait()
        scatter(i)

    def t_step(s, i, h):
        if s == 0:
            once(("back", i), lambda: back(i))
        t_send(s, i, h)

    def f_step(i):
        if i == 0:
            bulk(to.at[:, pl.ds(0, TM // 2 - 1)], one_recv.at[2])
        finish(i)

    run = {
        "k": tok_send, "a": a_send, "t": t_step, "w0": w0_step, "w1": w1_step, "w1b": w1b_step, "wp": wp_step,
        "wpb": wpb_step, "w3": w3_step, "act": act_spread, "sel": act_choose, "mask": build_mask, "t0": t0_step,
        "t1": t1_step, "q": spatial, "att": attend, "p": p_step, "r": renorm, "s": s_step, "m": mix, "f": f_step,
    }
    for name, *at in ORDER:
        run[name](*at)

    tok_drain()
    a_drain()
    t_drain()
    w0_drain()
    bulk(to.at[pl.ds(0, Z - 1), 0], one_send.at[1])
    bulk(to.at[:, pl.ds(0, TM // 2 - 1)], one_send.at[2])
    bulk(act.at[pl.ds(0, TM - 1)], one_send.at[3])
    bulk(actz.at[pl.ds(0, Z - 1)], one_send.at[4])
    for d in (0, 1):
        w1(d).wait_send()
        w1b(d).wait_send()
        for e in range(4):
            wp(e, d).wait_send()
            wpb(e, d).wait_send()
    for e in range(4):
        w3(e).wait_send()
    for i in range(CHUNKS):
        bulk(snd.at[i, pl.ds(0, TM - 1)], a2a_send.at[0, i])
        bulk(snd2.at[i, pl.ds(0, TM - 1)], a2a_send.at[1, i])


def body(
    tokens, action_rows, pair_index, episode_id, space_gain, space_qkv, space_out, time_gain, time_qkv, time_out
):
    hbm, vmem, smem = (pl.BlockSpec(memory_space=m) for m in (pltpu.HBM, pltpu.VMEM, pltpu.SMEM))
    dma = pltpu.SemaphoreType.DMA
    return pl.pallas_call(
        kernel,
        out_shape=jax.ShapeDtypeStruct(tokens.shape, BF),
        in_specs=[hbm, vmem, smem, smem, vmem, hbm, hbm, vmem, hbm, hbm],
        out_specs=vmem,
        scratch_shapes=[
            pltpu.VMEM((TOKENS, WIDTH), BF),
            pltpu.VMEM((TOKENS, WIDTH), BF),
            pltpu.VMEM((Z, CHUNKS, TM, PLACES, COLS), BF),
            pltpu.VMEM((3, WIDTH, COLS), BF),
            pltpu.VMEM((3, WIDTH, COLS), BF),
            pltpu.VMEM((2, 4, 4, Z, 128, 128), BF),
            pltpu.VMEM((Z, TM // 2, 16, COLS), BF),
            pltpu.VMEM((8, COLS), BF),
            pltpu.VMEM((TM, 8, COLS), BF),
            pltpu.VMEM((Z, 8, COLS), BF),
            pltpu.VMEM((8, WIDTH), F32),
            pltpu.VMEM((ROWS, WIDTH), BF),
            pltpu.VMEM((ROWS, WIDTH), F32),
            pltpu.VMEM((TOKENS, COLS), F32),
            pltpu.VMEM((3, TOKENS, COLS), BF),
            pltpu.VMEM((ROWS, ROWS), F32),
            pltpu.VMEM((CHUNKS, TM, PLACES, 3 * COLS), BF),
            pltpu.VMEM((CHUNKS, TM, PLACES, 3 * COLS), BF),
            pltpu.VMEM((CHUNKS, TM, PLACES, COLS), BF),
            pltpu.VMEM((CHUNKS, TM, PLACES, COLS), BF),
            dma((2, 4, CHUNKS, 2)),
            dma((2, 4, CHUNKS, 2)),
            dma((2, 4, CHUNKS, 2)),
            dma((2, 4, CHUNKS, 2)),
            dma((2, 4, CHUNKS, 2)),
            dma((2, 4, CHUNKS, 2)),
            dma((2, 4, 1, 2)),
            dma((2, 4, 1, 2)),
            dma((24,)),
            dma((24,)),
            dma((7,)),
            dma((5,)),
            dma((5,)),
            dma((2, CHUNKS)),
            dma((2, CHUNKS)),
        ],
        compiler_params=pltpu.CompilerParams(
            collective_id=0, has_side_effects=True, vmem_limit_bytes=60 * 1024 * 1024
        ),
    )(
        tokens, action_rows, pair_index, episode_id, space_gain.reshape(1, WIDTH), space_qkv, space_out,
        time_gain.reshape(1, WIDTH), time_qkv, time_out,
    )


def solution(mesh):
    return jax.shard_map(
        body,
        mesh=mesh,
        in_specs=(
            P("tm", None, "tensor"),
            P("tm", "tensor"),
            P("tm"),
            P(),
            P(),
            P(None, None, "tensor"),
            P("tensor", None),
            P(),
            P(None, None, "tensor"),
            P("tensor", None),
        ),
        out_specs=P("tm", None, "tensor"),
        check_vma=False,
    )
```

```python
import jax
import jax.numpy as jnp
from jax import lax
from jax.experimental import pallas as pl
from jax.experimental.pallas import tpu as pltpu
from jax.sharding import PartitionSpec as P

MESH = pl.DeviceIdType.MESH
HEAD_DIM = 128
EPSILON = 1e-06
SCALE = HEAD_DIM ** (-0.5)
TM, Z = 32, 8
CHUNKS, ROWS, COLS, WIDTH = 3, 256, 256, 2048
TOKENS = CHUNKS * ROWS
PLACES = ROWS // TM
BF, F32 = jnp.bfloat16, jnp.float32
ORDER = [
    ("w0", 0), ("act",), ("t0",), ("w0", 1), ("k", 0, 0, 0), ("mask",), ("k", 0, 0, 1), ("k", 0, 1, 0),
    ("k", 0, 1, 1), ("w0", 2), ("sel",), ("t1",), ("k", 1, 0, 0), ("k", 1, 0, 1), ("k", 1, 1, 0), ("k", 1, 1, 1),
    ("w0", 3), ("k", 2, 0, 0), ("k", 2, 0, 1), ("k", 2, 1, 0), ("k", 2, 1, 1), ("w1",), ("wp", 0), ("k", 0, 2, 0),
    ("k", 3, 0, 0), ("k", 3, 0, 1), ("k", 0, 2, 1), ("k", 3, 1, 0), ("k", 3, 1, 1), ("w1b",), ("wp", 1), ("wp", 2),
    ("k", 1, 2, 0), ("q", 0), ("k", 1, 2, 1), ("wpb", 0), ("q", 1), ("wp", 3), ("k", 2, 2, 0), ("k", 2, 2, 1),
    ("k", 3, 2, 0), ("wpb", 1), ("k", 3, 2, 1), ("q", 2), ("wpb", 2), ("att", 0), ("a", 0, 0, 0), ("a", 0, 0, 1),
    ("w3", 0), ("att", 1), ("a", 0, 1, 0), ("att", 2), ("a", 0, 1, 1), ("a", 1, 0, 0), ("wpb", 3), ("a", 1, 0, 1),
    ("w3", 1), ("a", 1, 1, 0), ("a", 1, 1, 1), ("w3", 2), ("a", 2, 0, 0), ("w3", 3), ("a", 2, 0, 1), ("a", 2, 1, 0),
    ("a", 2, 1, 1), ("a", 3, 0, 0), ("a", 3, 0, 1), ("a", 0, 2, 0), ("a", 3, 1, 0), ("a", 3, 1, 1), ("a", 0, 2, 1),
    ("p", 0, 0), ("p", 0, 1), ("a", 1, 2, 0), ("p", 0, 2), ("p", 0, 3), ("r", 0), ("a", 1, 2, 1), ("s", 0),
    ("a", 2, 2, 0), ("p", 1, 0), ("p", 1, 1), ("a", 2, 2, 1), ("p", 1, 2), ("p", 1, 3), ("a", 3, 2, 0), ("r", 1),
    ("a", 3, 2, 1), ("s", 1), ("p", 2, 0), ("p", 2, 1), ("m", 0), ("p", 2, 2), ("p", 2, 3), ("r", 2), ("s", 2),
    ("m", 1), ("t", 0, 0, 0), ("t", 0, 0, 1), ("t", 1, 0, 0), ("t", 1, 0, 1), ("t", 2, 0, 0), ("m", 2),
    ("t", 2, 0, 1), ("t", 0, 1, 0), ("t", 3, 0, 0), ("t", 0, 1, 1), ("t", 3, 0, 1), ("t", 1, 1, 0), ("t", 0, 2, 0),
    ("t", 1, 1, 1), ("f", 0), ("t", 0, 2, 1), ("t", 2, 1, 0), ("t", 1, 2, 0), ("t", 2, 1, 1), ("t", 1, 2, 1),
    ("t", 3, 1, 0), ("t", 2, 2, 0), ("t", 3, 1, 1), ("t", 2, 2, 1), ("t", 3, 2, 0), ("f", 1), ("t", 3, 2, 1),
    ("f", 2),
]


def kernel(
    tokens, action, pair, episode, space_gain, space_qkv, space_out, time_gain, time_qkv, time_out,
    out,
    tokf, af, tfb, wq, wt, wo, to, arow, act, actz, row, xn, mid, midz, qkv, mask, snd, rcv, snd2, rcv2,
    ring_ss, tok_rs, a_rs, t_rs, w0_rs, w_send, w_recv, loc, one_send, one_recv, a2a_send, a2a_recv,
):
    tm, z = lax.axis_index("tm"), lax.axis_index("tensor")
    y, x, k = tm // 8, lax.rem(tm // 2, 4), lax.rem(tm, 2)
    chip = tm // 2
    zr, zl = lax.rem(z + 1, Z), lax.rem(z + Z - 1, Z)

    def remote(src, dst, ssem, rsem, t, zz):
        return pltpu.make_async_remote_copy(
            src_ref=src, dst_ref=dst, send_sem=ssem, recv_sem=rsem, device_id=(t, zz), device_id_type=MESH
        )

    def bulk(ref, sem):
        pltpu.make_async_copy(ref, ref, sem).wait()

    def each(n, me, fn):
        def step(j, carry):
            fn(lax.rem(me + 1 + lax.rem(j + 9, n - 1), n))
            return carry
        lax.fori_loop(1, n, step, 0, unroll=True)

    own = pl.multiple_of(z * COLS, COLS)

    load_wq = pltpu.make_async_copy(space_qkv, wq, loc.at[0])
    load_wt = pltpu.make_async_copy(time_qkv, wt, loc.at[1])
    load_wq.start()
    load_wt.start()
    load_tok = pltpu.make_async_copy(tokens.at[0], tokf.at[:, pl.ds(own, COLS)], loc.at[2])
    load_tok.start()
    arow[...] = jnp.broadcast_to(action[...].astype(F32), (8, COLS)).astype(BF)

    barrier = pltpu.get_barrier_semaphore()
    each(TM, tm, lambda t: pl.semaphore_signal(barrier, inc=1, device_id=(t, z), device_id_type=MESH))
    each(Z, z, lambda q: pl.semaphore_signal(barrier, inc=1, device_id=(tm, q), device_id_type=MESH))
    pl.semaphore_wait(barrier, TM - 1 + Z - 1)

    seen = set()

    def once(key, wait):
        if key not in seen:
            seen.add(key)
            wait()

    def gather(name, view, first, ssem, rsem, chunks):
        def copy(d, s, i, h):
            origin = lax.rem(z + (Z - s if d == 0 else s), Z)
            dst = view(i, h, origin)
            src = first(i, h) if s == 0 else dst
            return remote(src, dst, ssem, rsem.at[d, s, i, h], tm, zr if d == 0 else zl)

        def arrived(d, s, i, h):
            once((name, d, s, i, h), lambda: copy(d, s, i, h).wait_recv())

        def send(s, i, h):
            for d in (0, 1):
                if s < 3 or h == d:
                    if s:
                        arrived(d, s - 1, i, h)
                    copy(d, s, i, h).start()

        def finish(i):
            for d in (0, 1):
                for s in range(4):
                    for h in (0, 1):
                        if s < 3 or h == d:
                            arrived(d, s, i, h)

        return send, finish

    HALF = ROWS // 2

    def flat(buf):
        def view(i, h, origin):
            return buf.at[
                pl.ds(ROWS * i + HALF * h, HALF), pl.ds(pl.multiple_of(origin * COLS, COLS), COLS)
            ]
        return view

    tok_send, tok_finish = gather(
        0, flat(tokf), lambda i, h: tokens.at[0, pl.ds(ROWS * i + HALF * h, HALF), :], ring_ss.at[0], tok_rs, CHUNKS
    )
    a_view = flat(af)
    a_send, a_finish = gather(1, a_view, lambda i, h: a_view(i, h, z), ring_ss.at[1], a_rs, CHUNKS)
    t_send, t_finish = gather(
        2, lambda i, h, origin: tfb.at[origin, i, pl.ds(h * (TM // 2), TM // 2)],
        lambda i, h: rcv2.at[i, pl.ds(h * (TM // 2), TM // 2)],
        ring_ss.at[2], t_rs, CHUNKS,
    )

    p, r = y + k * (x - y), x + k * (y - x)

    def place(pp, rr):
        return ((pp * 4 + rr) * (1 - k) + (rr * 4 + pp) * k) * 2 + k

    p1, p3 = lax.rem(p + 1, 4), lax.rem(p + 3, 4)
    r1, r3, r2 = lax.rem(r + 1, 4), lax.rem(r + 3, 4), lax.rem(r + 2, 4)
    w_src = space_out.at[pl.ds(pl.multiple_of(k * 128, 128), 128), pl.ds(pl.multiple_of(chip * 128, 128), 128)]

    w0_send, w0_finish = gather(
        3, lambda i, h, origin: wo.at[k, p, r, origin, pl.ds(64 * h, 64)],
        lambda i, h: space_out.at[
            pl.ds(pl.multiple_of(k * 128 + 64 * h, 64), 64), pl.ds(pl.multiple_of(chip * 128, 128), 128)
        ],
        ring_ss.at[3], w0_rs, 1,
    )
    w0_local = pltpu.make_async_copy(w_src, wo.at[k, p, r, z], loc.at[6])

    def w1(d):
        return remote(wo.at[k, p, r], wo.at[k, p, r], w_send.at[0], w_recv.at[d], place(p, r1 if d == 0 else r3), z)

    def w1b(d):
        ref = wo.at[k, p, r3 if d == 0 else r1, pl.ds(4 * d, 4)]
        return remote(ref, ref, w_send.at[0], w_recv.at[2 + d], place(p, r1 if d == 0 else r3), z)

    def wp(e, d):
        ref = wo.at[k, p, (r, r3, r1, r2)[e]]
        n = 4 + 2 * e + d
        return remote(ref, ref, w_send.at[1], w_recv.at[n], place(p1 if d == 0 else p3, r), z)

    def wpb(e, d):
        ref = wo.at[k, p3 if d == 0 else p1, (r, r3, r1, r2)[e], pl.ds(4 * d, 4)]
        n = 12 + 2 * e + d
        return remote(ref, ref, w_send.at[1], w_recv.at[n], place(p1 if d == 0 else p3, r), z)

    def w3(e):
        ref = wo.at[k, :, (r, r3, r1, r2)[e]]
        return remote(ref, ref, w_send.at[2], w_recv.at[20 + e], tm + 1 - 2 * k, z)

    def w_arrived(name, fn, *at):
        once((name, at), lambda: fn(*at).wait_recv())

    def t_src(q):
        return time_out.at[
            pl.ds(pl.multiple_of(chip * 16, 16), 16), pl.ds(pl.multiple_of(q * COLS, COLS), COLS)
        ]

    def t0(q):
        return remote(t_src(q), to.at[z, chip], one_send.at[1], one_recv.at[1], tm, q)

    def t0_local():
        return pltpu.make_async_copy(t_src(z), to.at[z, chip], one_recv.at[1])

    def t1(c):
        return remote(to.at[:, chip], to.at[:, chip], one_send.at[2], one_recv.at[2], c * 2 + k, z)

    def act_copy(t):
        return remote(arow, act.at[tm], one_send.at[3], one_recv.at[3], t, z)

    def actz_copy(q):
        return remote(actz.at[z], actz.at[z], one_send.at[4], one_recv.at[4], tm, q)

    def build_mask():
        one = lax.broadcasted_iota(jnp.int32, (ROWS, 128), 0)
        two = lax.broadcasted_iota(jnp.int32, (8, ROWS), 1)
        one_f, two_f = lax.shift_right_logical(one, 3), lax.shift_right_logical(two, 3)
        one_e, two_e = jnp.zeros_like(one), jnp.zeros_like(two)
        for f in range(TM):
            one_e = jnp.where(one_f == f, episode[f], one_e)
            two_e = jnp.where(two_f == f, episode[f], two_e)

        def wide_row(v):
            return jnp.concatenate([v, v], axis=1)

        def wide_col(v):
            return jnp.broadcast_to(v[0:1], (ROWS, ROWS))

        allowed = (
            (wide_row(one_e) == wide_col(two_e))
            & (wide_col(two_f) <= wide_row(one_f))
            & (wide_row(one & 7) == wide_col(two & 7))
        )
        mask[...] = jnp.where(allowed, 1.0, 0.0)

    STEP = 32

    def normed(get, gain):
        def tile(n, carry):
            at = pl.multiple_of(n * STEP, STEP)
            v = get(at)
            factor = lax.rsqrt(jnp.sum(v * v, -1, keepdims=True) * (1.0 / WIDTH) + EPSILON)
            xn[pl.ds(at, STEP), :] = (v * factor * gain[...]).astype(BF)
            return carry
        lax.fori_loop(0, ROWS // STEP, tile, 0)

    def spatial(i):
        if i == 0:
            load_wq.wait()
            load_tok.wait()
            bulk(actz.at[pl.ds(0, Z - 1)], one_recv.at[4])
            for q in range(Z):
                row[:, COLS * q : COLS * (q + 1)] = actz[q].astype(F32)
        tok_finish(i)

        def start_tile(at):
            return tokf[pl.ds(ROWS * i + at, STEP), :].astype(F32) + row[0:1, :]

        normed(start_tile, space_gain)
        for n in range(3):
            qkv[n, ROWS * i : ROWS * (i + 1), :] = jnp.dot(xn[...], wq[n], preferred_element_type=F32).astype(BF)

    def attend(i):
        for h in range(2):
            cols = slice(HEAD_DIM * h, HEAD_DIM * (h + 1))
            s = lax.dot_general(
                qkv[0, ROWS * i : ROWS * (i + 1), cols], qkv[1, :, cols], (((1,), (1,)), ((), ())),
                preferred_element_type=F32,
            ) * SCALE
            e = jnp.exp(s - jnp.max(s, -1, keepdims=True))
            prob = (e / jnp.sum(e, -1, keepdims=True)).astype(BF)
            o = jnp.dot(prob, qkv[2, :, cols], preferred_element_type=F32)
            at = pl.multiple_of(z * COLS + HEAD_DIM * h, HEAD_DIM)
            af[ROWS * i : ROWS * (i + 1), pl.ds(at, HEAD_DIM)] = o.astype(BF)

    def project(i, lo, hi):
        rows = slice(ROWS * i, ROWS * (i + 1))

        def tile(j, carry):
            yy, xx = j // 2, 2 * lax.rem(j, 2)

            def rhs(kk):
                a, b = ((yy, xx), (yy, xx + 1)) if kk == 0 else ((xx, yy), (xx + 1, yy))
                return jnp.concatenate(
                    [wo[kk, a[0], a[1]].reshape(1024, 128), wo[kk, b[0], b[1]].reshape(1024, 128)], axis=1
                )

            def lhs(kk):
                return jnp.concatenate(
                    [af[rows, COLS * q + 128 * kk : COLS * q + 128 * (kk + 1)] for q in range(Z)], axis=1
                )

            at = pl.multiple_of(j * COLS, COLS)
            total = jnp.dot(lhs(0), rhs(0), preferred_element_type=F32)
            total = total + jnp.dot(lhs(1), rhs(1), preferred_element_type=F32)
            start = tokf[rows, pl.ds(at, COLS)].astype(F32) + row[0:1, pl.ds(at, COLS)]
            mid[:, pl.ds(at, COLS)] = start + total
            return carry
        lax.fori_loop(lo, hi, tile, 0)

    def renorm(i):
        normed(lambda at: mid[pl.ds(at, STEP), :], time_gain)
        midz[ROWS * i : ROWS * (i + 1), :] = mid[:, pl.ds(own, COLS)]

    def qkv_copy(i, t):
        return remote(snd.at[i, t], rcv.at[i, tm], a2a_send.at[0, i], a2a_recv.at[0, i], t, z)

    def scatter(i):
        for n in range(3):
            v = jnp.dot(xn[...], wt[n], preferred_element_type=F32)
            snd[i, :, :, COLS * n : COLS * (n + 1)] = v.reshape(TM, PLACES, COLS).astype(BF)
        each(TM, tm, lambda t: qkv_copy(i, t).start())
        pltpu.make_async_copy(snd.at[i, tm], rcv.at[i, tm], a2a_recv.at[0, i]).start()

    def mix_copy(i, t):
        return remote(snd2.at[i, t], rcv2.at[i, tm], a2a_send.at[1, i], a2a_recv.at[1, i], t, z)

    def mix(i):
        bulk(rcv.at[i], a2a_recv.at[0, i])

        def take(n, h):
            at = COLS * n + HEAD_DIM * h
            return rcv[i, :, :, at : at + HEAD_DIM].astype(F32).reshape(ROWS, HEAD_DIM).astype(BF)

        for h in range(2):
            s = lax.dot_general(
                take(0, h), take(1, h), (((1,), (1,)), ((), ())), preferred_element_type=F32
            ) * SCALE
            s = jnp.where(mask[...] > 0.5, s, -1e30)
            e = jnp.exp(s - jnp.max(s, -1, keepdims=True))
            prob = (e / jnp.sum(e, -1, keepdims=True)).astype(BF)
            o = jnp.dot(prob, take(2, h), preferred_element_type=F32)
            snd2[i, :, :, HEAD_DIM * h : HEAD_DIM * (h + 1)] = o.reshape(TM, PLACES, HEAD_DIM).astype(BF)
        each(TM, tm, lambda t: mix_copy(i, t).start())
        pltpu.make_async_copy(snd2.at[i, tm], rcv2.at[i, tm], a2a_recv.at[1, i]).start()

    def back(i):
        bulk(rcv2.at[i], a2a_recv.at[1, i])
        pltpu.make_async_copy(rcv2.at[i], tfb.at[z, i], loc.at[3 + i]).start()

    def finish(i):
        t_finish(i)
        pltpu.make_async_copy(rcv2.at[i], tfb.at[z, i], loc.at[3 + i]).wait()
        lhs = jnp.concatenate([tfb[q, i].astype(F32).reshape(ROWS, COLS).astype(BF) for q in range(Z)], axis=1)
        update = jnp.dot(lhs, to[...].reshape(WIDTH, COLS), preferred_element_type=F32)
        rows = slice(ROWS * i, ROWS * (i + 1))
        out[0, rows, :] = (midz[rows, :] + update).astype(BF)

    def act_spread():
        each(TM, tm, lambda t: act_copy(t).start())
        pltpu.make_async_copy(arow, act.at[tm], one_recv.at[3]).start()

    def act_choose():
        bulk(act, one_recv.at[3])
        actz[z] = act[pair[0]]
        each(Z, z, lambda q: actz_copy(q).start())

    def w0_step(s):
        if s == 0:
            w0_local.start()
        for h in (0, 1):
            w0_send(s, 0, h)

    def w1_step():
        w0_finish(0)
        w0_local.wait()
        w1(0).start()
        w1(1).start()

    def w1b_step():
        for d in (0, 1):
            w_arrived("w1", w1, d)
            w1b(d).start()

    def wp_step(e):
        if e in (1, 2):
            w_arrived("w1", w1, e - 1)
        if e == 3:
            w_arrived("w1b", w1b, 0)
            w_arrived("w1b", w1b, 1)
        wp(e, 0).start()
        wp(e, 1).start()

    def wpb_step(e):
        for d in (0, 1):
            w_arrived("wp", wp, e, d)
            wpb(e, d).start()

    def w3_step(e):
        for d in (0, 1):
            w_arrived("wpb", wpb, e, d)
        w3(e).start()

    def t0_step():
        each(Z, z, lambda q: t0(q).start())
        t0_local().start()

    def t1_step():
        bulk(to.at[:, 0], one_recv.at[1])
        each(TM // 2, chip, lambda c: t1(c).start())

    def p_step(i, j):
        if j == 0:
            for e in range(4):
                w_arrived("w3", w3, e)
            a_finish(i)
        project(i, 2 * j, 2 * j + 2)

    def s_step(i):
        if i == 0:
            load_wt.wait()
        scatter(i)

    def t_step(s, i, h):
        if s == 0:
            once(("back", i), lambda: back(i))
        t_send(s, i, h)

    def f_step(i):
        if i == 0:
            bulk(to.at[:, pl.ds(0, TM // 2 - 1)], one_recv.at[2])
        finish(i)

    run = {
        "k": tok_send, "a": a_send, "t": t_step, "w0": w0_step, "w1": w1_step, "w1b": w1b_step, "wp": wp_step,
        "wpb": wpb_step, "w3": w3_step, "act": act_spread, "sel": act_choose, "mask": build_mask, "t0": t0_step,
        "t1": t1_step, "q": spatial, "att": attend, "p": p_step, "r": renorm, "s": s_step, "m": mix, "f": f_step,
    }
    for name, *at in ORDER:
        run[name](*at)

    sent = WIDTH - COLS
    bulk(tokf.at[:, pl.ds(0, sent)], ring_ss.at[0])
    bulk(af.at[:, pl.ds(0, sent)], ring_ss.at[1])
    bulk(tfb.at[pl.ds(0, Z - 1)], ring_ss.at[2])
    bulk(wo.at[0, 0, 0, pl.ds(0, Z - 1)], ring_ss.at[3])
    bulk(to.at[pl.ds(0, Z - 1), 0], one_send.at[1])
    bulk(to.at[:, pl.ds(0, TM // 2 - 1)], one_send.at[2])
    bulk(act.at[pl.ds(0, TM - 1)], one_send.at[3])
    bulk(actz.at[pl.ds(0, Z - 1)], one_send.at[4])
    bulk(wo.at[0, 0, pl.ds(0, 3)], w_send.at[0])
    bulk(wo.at[0, pl.ds(0, 3)], w_send.at[1])
    bulk(wo.at[0], w_send.at[2])
    for i in range(CHUNKS):
        bulk(snd.at[i, pl.ds(0, TM - 1)], a2a_send.at[0, i])
        bulk(snd2.at[i, pl.ds(0, TM - 1)], a2a_send.at[1, i])


def body(
    tokens, action_rows, pair_index, episode_id, space_gain, space_qkv, space_out, time_gain, time_qkv, time_out
):
    hbm, vmem, smem = (pl.BlockSpec(memory_space=m) for m in (pltpu.HBM, pltpu.VMEM, pltpu.SMEM))
    dma = pltpu.SemaphoreType.DMA
    return pl.pallas_call(
        kernel,
        out_shape=jax.ShapeDtypeStruct(tokens.shape, BF),
        in_specs=[hbm, vmem, smem, smem, vmem, hbm, hbm, vmem, hbm, hbm],
        out_specs=vmem,
        scratch_shapes=[
            pltpu.VMEM((TOKENS, WIDTH), BF),
            pltpu.VMEM((TOKENS, WIDTH), BF),
            pltpu.VMEM((Z, CHUNKS, TM, PLACES, COLS), BF),
            pltpu.VMEM((3, WIDTH, COLS), BF),
            pltpu.VMEM((3, WIDTH, COLS), BF),
            pltpu.VMEM((2, 4, 4, Z, 128, 128), BF),
            pltpu.VMEM((Z, TM // 2, 16, COLS), BF),
            pltpu.VMEM((8, COLS), BF),
            pltpu.VMEM((TM, 8, COLS), BF),
            pltpu.VMEM((Z, 8, COLS), BF),
            pltpu.VMEM((8, WIDTH), F32),
            pltpu.VMEM((ROWS, WIDTH), BF),
            pltpu.VMEM((ROWS, WIDTH), F32),
            pltpu.VMEM((TOKENS, COLS), F32),
            pltpu.VMEM((3, TOKENS, COLS), BF),
            pltpu.VMEM((ROWS, ROWS), F32),
            pltpu.VMEM((CHUNKS, TM, PLACES, 3 * COLS), BF),
            pltpu.VMEM((CHUNKS, TM, PLACES, 3 * COLS), BF),
            pltpu.VMEM((CHUNKS, TM, PLACES, COLS), BF),
            pltpu.VMEM((CHUNKS, TM, PLACES, COLS), BF),
            dma((4,)),
            dma((2, 4, CHUNKS, 2)),
            dma((2, 4, CHUNKS, 2)),
            dma((2, 4, CHUNKS, 2)),
            dma((2, 4, 1, 2)),
            dma((3,)),
            dma((24,)),
            dma((7,)),
            dma((5,)),
            dma((5,)),
            dma((2, CHUNKS)),
            dma((2, CHUNKS)),
        ],
        compiler_params=pltpu.CompilerParams(
            collective_id=0, has_side_effects=True, vmem_limit_bytes=60 * 1024 * 1024
        ),
    )(
        tokens, action_rows, pair_index, episode_id, space_gain.reshape(1, WIDTH), space_qkv, space_out,
        time_gain.reshape(1, WIDTH), time_qkv, time_out,
    )


def solution(mesh):
    return jax.shard_map(
        body,
        mesh=mesh,
        in_specs=(
            P("tm", None, "tensor"),
            P("tm", "tensor"),
            P("tm"),
            P(),
            P(),
            P(None, None, "tensor"),
            P("tensor", None),
            P(),
            P(None, None, "tensor"),
            P("tensor", None),
        ),
        out_specs=P("tm", None, "tensor"),
        check_vma=False,
    )
```
